32 devices in a mesh: dp: 4 (over z), seq: 2 (over core), tensor: 4 (over y, x).
Axes of the slice: x: 2, y: 2, z: 4, core: 2. Of those that a mesh axis runs over, the one named last changes fastest.
Arguments:
- block_input: bfloat16 [1024, 1024], P(('dp', 'seq')), may hold values from -6 to 6
- norm1_gain: float32 [1024], replicated, may hold values from 0.5 to 1.5
- q_weight: bfloat16 [1024, 768], replicated, may hold values from -0.1875 to 0.1875
- k_weight: bfloat16 [1024, 768], replicated, may hold values from -0.1875 to 0.1875
- v_weight: bfloat16 [1024, 6, 256], P(None, None, 'tensor'), may hold values from -0.1875 to 0.1875
- gate_weight: bfloat16 [1024, 6, 256], P(None, None, 'tensor'), may hold values from -0.1875 to 0.1875
- beta_weight: bfloat16 [1024, 6], replicated, may hold values from -0.1875 to 0.1875
- decay_weight: bfloat16 [1024, 6], replicated, may hold values from -0.1875 to 0.1875
- q_conv: float32 [4, 768], replicated, may hold values from -3 to 3
- k_conv: float32 [4, 768], replicated, may hold values from -3 to 3
- v_conv: float32 [4, 6, 256], P(None, None, 'tensor'), may hold values from -3 to 3
- decay_scale: float32 [6], replicated, may hold values from 0.0009765625 to 0.05
- dt_bias: float32 [6], replicated, may hold values from -1 to 1
- out_gain: float32 [256], P('tensor'), may hold values from 0.5 to 1.5
- out_weight: bfloat16 [6, 256, 1024], P(None, 'tensor'), may hold values from -0.3125 to 0.3125
- norm2_gain: float32 [1024], replicated, may hold values from 0.5 to 1.5
- ffn_gate: bfloat16 [1024, 2816], P(None, 'tensor'), may hold values from -0.1875 to 0.1875
- ffn_up: bfloat16 [1024, 2816], P(None, 'tensor'), may hold values from -0.1875 to 0.1875
- ffn_down: bfloat16 [2816, 1024], P('tensor'), may hold values from -0.109375 to 0.109375
- cotangent: bfloat16 [1024, 1024], P(('dp', 'seq')), may hold values from -6 to 6
Outputs:
- block_output: bfloat16 [1024, 1024], P(('dp', 'seq'))
- grad_input: float32 [1024, 1024], P(('dp', 'seq'))
- grad_norm1_gain: float32 [1024], replicated
- grad_q_weight: float32 [1024, 768], replicated
- grad_k_weight: float32 [1024, 768], replicated
- grad_v_weight: float32 [1024, 6, 256], P(None, None, 'tensor')
- grad_gate_weight: float32 [1024, 6, 256], P(None, None, 'tensor')
- grad_beta_weight: float32 [1024, 6], replicated
- grad_decay_weight: float32 [1024, 6], replicated
- grad_q_conv: float32 [4, 768], replicated
- grad_k_conv: float32 [4, 768], replicated
- grad_v_conv: float32 [4, 6, 256], P(None, None, 'tensor')
- grad_decay_scale: float32 [6], replicated
- grad_dt_bias: float32 [6], replicated
- grad_out_gain: float32 [256], P('tensor')
- grad_out_weight: float32 [6, 256, 1024], P(None, 'tensor')
- grad_norm2_gain: float32 [1024], replicated
- grad_ffn_gate: float32 [1024, 2816], P(None, 'tensor')
- grad_ffn_up: float32 [1024, 2816], P(None, 'tensor')
- grad_ffn_down: float32 [2816, 1024], P('tensor')
The draws below stay inside these ranges and needn't reach their ends.
All inputs are finite; a program needn't handle non-finite values.
Results may differ from the reference program's by a relative error of at most 0.025.
Values may be sent and summed in bfloat16 or wider, within the bound.
No kernel may reach another device: no remote copies, remote signals or barrier semaphores. Data moves between devices by JAX's collectives and lax.ppermute only.
A program may use at most 128 MiB of HBM per device.

```python
import math
import jax
import jax.numpy as jnp
from jax import lax

D = 1024
H = 6
DK = 128
DV = 256
FF = 2816
CONV = 4
SPAN = 64
LEN = 256
SEQS = 4
TOKENS = 1024
N_TENSOR = 4


def block_levels(stream_key, extent, shards, low, high):
    def one(axis_at, parts):
        draws = jax.random.uniform(jax.random.fold_in(jax.random.fold_in(stream_key, 6), axis_at), (parts,), jnp.float32, low / len(shards), high / len(shards))
        return jnp.repeat(jnp.exp(draws), extent[axis_at] // parts).reshape((-1,) + (1,) * (len(extent) - axis_at - 1))

    level = one(*shards[0])
    for cut in shards[1:]:
        level = level * one(*cut)
    return level


def normal_values(stream_key, shape, spread, reach, pieces=(), kind=jnp.bfloat16):
    level = block_levels(stream_key, shape, pieces, -0.22, 0.18) if pieces else 1.0
    values = jax.random.normal(stream_key, shape, jnp.float32) * spread * level
    return jnp.minimum(jnp.maximum(values, -reach), reach).astype(kind)


def setup_inputs(seed: int = 0) -> dict:
    seeds = jax.random.split(jax.random.key(seed), 21)
    return {
        "block_input": normal_values(seeds[0], (TOKENS, D), 1.0, 6.0, ((0, 8),)),
        "norm1_gain": jnp.clip(1.0 + 0.1 * jax.random.normal(seeds[1], (D,), jnp.float32), 0.5, 1.5),
        "q_weight": normal_values(seeds[2], (D, H * DK), D ** -0.5, 0.1875),
        "k_weight": normal_values(seeds[3], (D, H * DK), D ** -0.5, 0.1875),
        "v_weight": normal_values(seeds[4], (D, H, DV), D ** -0.5, 0.1875, ((2, 4),)),
        "gate_weight": normal_values(seeds[5], (D, H, DV), D ** -0.5, 0.1875, ((2, 4),)),
        "beta_weight": normal_values(seeds[6], (D, H), D ** -0.5, 0.1875),
        "decay_weight": normal_values(seeds[7], (D, H), D ** -0.5, 0.1875),
        "q_conv": normal_values(seeds[8], (CONV, H * DK), 0.5, 3.0, (), jnp.float32),
        "k_conv": normal_values(seeds[9], (CONV, H * DK), 0.5, 3.0, (), jnp.float32),
        "v_conv": normal_values(seeds[10], (CONV, H, DV), 0.5, 3.0, ((2, 4),), jnp.float32),
        "decay_scale": jnp.clip(jnp.exp(jax.random.uniform(seeds[11], (H,), jnp.float32, math.log(0.0009765625), math.log(0.05))), 0.0009765625, 0.05),
        "dt_bias": jnp.clip(jax.random.uniform(seeds[12], (H,), jnp.float32, -1.0, 1.0), -1.0, 1.0),
        "out_gain": jnp.clip(1.0 + 0.1 * jax.random.normal(seeds[13], (DV,), jnp.float32), 0.5, 1.5),
        "out_weight": normal_values(seeds[14], (H, DV, D), (H * DV // 4) ** -0.5, 0.3125, ((1, 4),)),
        "norm2_gain": jnp.clip(1.0 + 0.1 * jax.random.normal(seeds[15], (D,), jnp.float32), 0.5, 1.5),
        "ffn_gate": normal_values(seeds[16], (D, FF), D ** -0.5, 0.1875, ((1, 4),)),
        "ffn_up": normal_values(seeds[17], (D, FF), D ** -0.5, 0.1875, ((1, 4),)),
        "ffn_down": normal_values(seeds[18], (FF, D), FF ** -0.5, 0.109375, ((0, 4),)),
        "cotangent": normal_values(seeds[19], (TOKENS, D), 1.0, 6.0, ((0, 8),)),
    }


EPS = 1e-06
HIGH_PRECISION = lax.Precision.HIGHEST

def matmul(left, right):
    return jnp.dot(left.astype(jnp.float32), right.astype(jnp.float32), preferred_element_type=jnp.float32)

def rounded(matrix):
    return lax.optimization_barrier(matrix.astype(jnp.bfloat16)).astype(jnp.float32)

def rms_scale(matrix, gain):
    return matrix * lax.rsqrt(lax.optimization_barrier(jnp.mean(matrix * matrix, axis=-1, keepdims=True)) + EPS) * gain

def swiglu(gate_act, up_act):
    return jax.nn.silu(gate_act) * up_act

def conv_silu(edge_rows, rows, conv_taps):
    length = rows.shape[0]
    padded = jnp.concatenate([edge_rows, rows], axis=0)
    summed = conv_taps[0] * padded[0:length]
    for offset in range(1, conv_taps.shape[0]):
        summed = summed + conv_taps[offset] * padded[offset:offset + length]
    return jax.nn.silu(summed)

def unit_rows(matrix):
    return matrix * lax.rsqrt(lax.optimization_barrier(jnp.sum(matrix * matrix, axis=-1, keepdims=True)) + EPS)

def mixer_inputs(q_proj, k_proj, v_proj, b_proj, a_proj, q_edge, k_edge, v_edge, q_conv, k_conv, v_conv, decay_scale, dt_bias):
    length = q_proj.shape[0]
    n_heads = b_proj.shape[1]
    queries = conv_silu(q_edge, q_proj, q_conv).reshape(length, n_heads, -1)
    key_vecs = conv_silu(k_edge, k_proj, k_conv).reshape(length, n_heads, -1)
    values = conv_silu(v_edge, v_proj, v_conv.reshape(v_conv.shape[0], -1)).reshape(length, n_heads, -1)
    queries = unit_rows(queries) * queries.shape[2] ** (-0.5)
    key_vecs = unit_rows(key_vecs)
    beta_gate = jax.nn.sigmoid(b_proj)
    log_decay = -decay_scale * jax.nn.softplus(a_proj + dt_bias)
    return (jnp.transpose(queries, (1, 0, 2)), jnp.transpose(key_vecs, (1, 0, 2)), jnp.transpose(values, (1, 0, 2)), beta_gate.T, log_decay.T)

def gated_norm(head_out, gate_proj, gain, sum_squares):
    scale_rows = lax.rsqrt(sum_squares / DV + EPS)[..., None]
    return head_out * scale_rows * gain * jax.nn.silu(gate_proj)

def delta_run(queries, key_vecs, values, beta_gate, log_decay, start_state):
    n_heads, length, key_width = key_vecs.shape
    val_width = values.shape[2]
    n_blocks = length // SPAN
    q_blk = queries.reshape(n_heads, n_blocks, SPAN, key_width)
    k_blk = key_vecs.reshape(n_heads, n_blocks, SPAN, key_width)
    v_blk = values.reshape(n_heads, n_blocks, SPAN, val_width)
    b_blk = beta_gate.reshape(n_heads, n_blocks, SPAN)
    g_cum = jnp.cumsum(log_decay.reshape(n_heads, n_blocks, SPAN), axis=-1)
    places = jnp.arange(SPAN)
    strict = places[:, None] > places[None, :]
    within = places[:, None] >= places[None, :]
    differ = g_cum[..., :, None] - g_cum[..., None, :]
    decays = jnp.where(within, jnp.exp(jnp.where(within, differ, 0.0)), 0.0)
    k_gram = jnp.einsum('hnik,hnjk->hnij', k_blk, k_blk, precision=HIGH_PRECISION)
    l_mat = jnp.eye(SPAN, dtype=jnp.float32) + jnp.where(strict, b_blk[..., :, None] * k_gram * decays, 0.0)
    right_side = jnp.concatenate([b_blk[..., None] * v_blk, (b_blk * jnp.exp(g_cum))[..., None] * k_blk], axis=-1)
    solved = lax.linalg.triangular_solve(l_mat, right_side, left_side=True, lower=True, unit_diagonal=True)
    updates = solved[..., :val_width]
    w_mat = solved[..., val_width:]
    qk_mat = jnp.einsum('hnik,hnjk->hnij', q_blk, k_blk, precision=HIGH_PRECISION) * decays
    g_last = g_cum[..., -1:]
    k_end = k_blk * jnp.exp(g_last - g_cum)[..., None]
    q_dec = q_blk * jnp.exp(g_cum)[..., None]

    def advance(current_state, block_in):
        current_update_rows, current_write_rows, current_query_decayed, current_query_key, current_key_edge, current_gate_log = block_in
        fresh_value_rows = current_update_rows - jnp.einsum('nsz,nzu->nsu', current_write_rows, current_state, precision=HIGH_PRECISION)
        block_result = jnp.einsum('nsz,nzu->nsu', current_query_decayed, current_state, precision=HIGH_PRECISION) + jnp.einsum('zdn,znb->zdb', current_query_key, fresh_value_rows, precision=HIGH_PRECISION)
        following_state = jnp.exp(current_gate_log)[..., None] * current_state + jnp.einsum('ozq,ozp->oqp', current_key_edge, fresh_value_rows, precision=HIGH_PRECISION)
        return (following_state, block_result)
    blocks_in = tuple((jnp.moveaxis(member, 1, 0) for member in (updates, w_mat, q_dec, qk_mat, k_end, g_last)))
    final_state, outputs = lax.scan(advance, start_state, blocks_in)
    return (jnp.moveaxis(outputs, 0, 1).reshape(n_heads, length, val_width), final_state)

def one_sequence(inputs, cot_rows, params):
    norm1_gain, q_weight, k_weight, v_weight, gate_weight, beta_weight, decay_weight, q_conv, k_conv, v_conv, decay_scale, dt_bias, out_gain, out_weight, norm2_gain, ffn_gate, ffn_up, ffn_down = params
    value_part = DV // N_TENSOR
    ffn_part = FF // N_TENSOR
    edge_count = CONV - 1
    inputs_f = inputs.astype(jnp.float32)
    normed1, pull_norm1 = jax.vjp(rms_scale, inputs_f, norm1_gain)
    normed1_b = normed1.astype(jnp.bfloat16)
    q_proj = matmul(normed1_b, q_weight)
    k_proj = matmul(normed1_b, k_weight)
    b_proj = matmul(normed1_b, beta_weight)
    a_proj = matmul(normed1_b, decay_weight)
    zero_qk = jnp.zeros((edge_count, H * DK), jnp.float32)
    zero_val = jnp.zeros((edge_count, H * value_part), jnp.float32)

    def prepare(qp_in, kp_in, vp_in, bp_in, ap_in, qc_in, kc_in, vc_in, ds_in, db_in):
        return mixer_inputs(qp_in, kp_in, vp_in, bp_in, ap_in, zero_qk, zero_qk, zero_val, qc_in, kc_in, vc_in, ds_in, db_in)
    v_mats, g_mats, gate_projs, pulls_in, pulls_delta, head_outs = ([], [], [], [], [], [])
    for group_index in range(N_TENSOR):
        first_chan = group_index * value_part
        v_mat = v_weight[:, :, first_chan:first_chan + value_part].reshape(D, -1)
        g_mat = gate_weight[:, :, first_chan:first_chan + value_part].reshape(D, -1)
        v_proj = matmul(normed1_b, v_mat)
        gate_proj = matmul(normed1_b, g_mat).reshape(LEN, H, value_part)
        prepared, pull_inputs = jax.vjp(prepare, q_proj, k_proj, v_proj, b_proj, a_proj, q_conv, k_conv, v_conv[:, :, first_chan:first_chan + value_part], decay_scale, dt_bias)
        queries, key_vecs, values, beta_gate, log_decay = prepared
        (mixed_heads, final_state), pull_delta = jax.vjp(delta_run, queries, key_vecs, values, beta_gate, log_decay, jnp.zeros((H, DK, value_part), jnp.float32))
        v_mats.append(v_mat)
        g_mats.append(g_mat)
        gate_projs.append(gate_proj)
        pulls_in.append(pull_inputs)
        pulls_delta.append((pull_delta, final_state))
        head_outs.append(jnp.transpose(mixed_heads, (1, 0, 2)))
    sum_squares = head_outs[0].sum(axis=2) * 0.0
    for group_index in range(N_TENSOR):
        sum_squares = sum_squares + lax.optimization_barrier(jnp.sum(head_outs[group_index] * head_outs[group_index], axis=2))
    mixer_total = jnp.zeros((LEN, D), jnp.float32)
    gated_list, pulls_gate, o_mats = ([], [], [])
    for group_index in range(N_TENSOR):
        first_chan = group_index * value_part
        gated, pull_gate = jax.vjp(gated_norm, head_outs[group_index], gate_projs[group_index], out_gain[first_chan:first_chan + value_part], sum_squares)
        gated_b = gated.astype(jnp.bfloat16).reshape(LEN, -1)
        o_mat = out_weight[:, first_chan:first_chan + value_part, :].reshape(-1, D)
        mixer_total = mixer_total + rounded(matmul(gated_b, o_mat))
        gated_list.append(gated_b)
        pulls_gate.append(pull_gate)
        o_mats.append(o_mat)
    hidden_res = inputs_f + mixer_total
    normed2, pull_norm2 = jax.vjp(rms_scale, hidden_res, norm2_gain)
    normed2_b = normed2.astype(jnp.bfloat16)
    ffn_total = jnp.zeros((LEN, D), jnp.float32)
    ffn_store = []
    for group_index in range(N_TENSOR):
        first_unit = group_index * ffn_part
        gate_mat = ffn_gate[:, first_unit:first_unit + ffn_part]
        up_mat = ffn_up[:, first_unit:first_unit + ffn_part]
        down_mat = ffn_down[first_unit:first_unit + ffn_part, :]
        inner, pull_ffn = jax.vjp(swiglu, matmul(normed2_b, gate_mat), matmul(normed2_b, up_mat))
        inner_b = inner.astype(jnp.bfloat16)
        ffn_total = ffn_total + rounded(matmul(inner_b, down_mat))
        ffn_store.append((gate_mat, up_mat, down_mat, inner_b, pull_ffn))
    block_output = (hidden_res + ffn_total).astype(jnp.bfloat16)
    grad_normed2 = jnp.zeros((LEN, D), jnp.float32)
    g_gate_list, g_up_list, g_down_list = ([], [], [])
    for group_index in range(N_TENSOR):
        gate_mat, up_mat, down_mat, inner_b, pull_ffn = ffn_store[group_index]
        grad_inner = matmul(cot_rows, down_mat.T)
        g_down_list.append(matmul(inner_b.T, cot_rows))
        grad_gate_act, grad_up_act = pull_ffn(grad_inner)
        gate_grad_b = grad_gate_act.astype(jnp.bfloat16)
        up_grad_b = grad_up_act.astype(jnp.bfloat16)
        g_gate_list.append(matmul(normed2_b.T, gate_grad_b))
        g_up_list.append(matmul(normed2_b.T, up_grad_b))
        grad_normed2 = grad_normed2 + rounded(matmul(gate_grad_b, gate_mat.T) + matmul(up_grad_b, up_mat.T))
    grad_hidden_n, grad_norm2 = pull_norm2(grad_normed2)
    grad_hidden = cot_rows.astype(jnp.float32) + grad_hidden_n
    grad_hidden_b = grad_hidden.astype(jnp.bfloat16)
    g_out_list, g_gain_list, gate_back, heads_back = ([], [], [], [])
    grad_squares = jnp.zeros((LEN, H), jnp.float32)
    for group_index in range(N_TENSOR):
        grad_gated = matmul(grad_hidden_b, o_mats[group_index].T).reshape(LEN, H, value_part)
        g_out_list.append(matmul(gated_list[group_index].T, grad_hidden_b).reshape(H, value_part, D))
        heads_local, grad_gate_proj, grad_gain_part, squares_part = pulls_gate[group_index](grad_gated)
        grad_squares = grad_squares + squares_part
        g_gain_list.append(grad_gain_part)
        gate_back.append(grad_gate_proj)
        heads_back.append(heads_local)
    shared = [jnp.zeros(member.shape, jnp.float32) for member in (q_weight, k_weight, beta_weight, decay_weight, q_conv, k_conv, decay_scale, dt_bias, norm1_gain)]
    g_v_list, g_g_list, g_vc_list = ([], [], [])
    grad_input_sum = jnp.zeros((LEN, D), jnp.float32)
    for group_index in range(N_TENSOR):
        grad_heads = heads_back[group_index] + 2.0 * head_outs[group_index] * grad_squares[..., None]
        pull_delta, final_state = pulls_delta[group_index]
        delta_grads = pull_delta((jnp.transpose(grad_heads, (1, 0, 2)), jnp.zeros_like(final_state)))
        input_grads = pulls_in[group_index]((delta_grads[0], delta_grads[1], delta_grads[2], delta_grads[3], delta_grads[4]))
        qg_b = input_grads[0].astype(jnp.bfloat16)
        kg_b = input_grads[1].astype(jnp.bfloat16)
        vg_b = input_grads[2].astype(jnp.bfloat16)
        bg_b = input_grads[3].astype(jnp.bfloat16)
        ag_b = input_grads[4].astype(jnp.bfloat16)
        gg_b = gate_back[group_index].reshape(LEN, -1).astype(jnp.bfloat16)
        normed1_part = matmul(qg_b, q_weight.T) + matmul(kg_b, k_weight.T) + matmul(vg_b, v_mats[group_index].T) + matmul(gg_b, g_mats[group_index].T) + matmul(bg_b, beta_weight.T) + matmul(ag_b, decay_weight.T)
        grad_input_n, grad_norm1 = pull_norm1(normed1_part)
        grad_input_sum = grad_input_sum + rounded(grad_input_n)
        terms = (matmul(normed1_b.T, qg_b), matmul(normed1_b.T, kg_b), matmul(normed1_b.T, bg_b), matmul(normed1_b.T, ag_b), input_grads[5], input_grads[6], input_grads[8], input_grads[9], grad_norm1)
        shared = [shared[member] + terms[member] for member in range(9)]
        g_v_list.append(matmul(normed1_b.T, vg_b).reshape(D, H, value_part))
        g_g_list.append(matmul(normed1_b.T, gg_b).reshape(D, H, value_part))
        g_vc_list.append(input_grads[7])
    grad_input = grad_hidden + grad_input_sum
    grads = (shared[8], shared[0], shared[1], jnp.concatenate(g_v_list, axis=2), jnp.concatenate(g_g_list, axis=2), shared[2], shared[3], shared[4], shared[5], jnp.concatenate(g_vc_list, axis=2), shared[6], shared[7], jnp.concatenate(g_gain_list, axis=0), jnp.concatenate(g_out_list, axis=1), grad_norm2, jnp.concatenate(g_gate_list, axis=1), jnp.concatenate(g_up_list, axis=1), jnp.concatenate(g_down_list, axis=0))
    return (block_output, grad_input, grads)

def reference(block_input, norm1_gain, q_weight, k_weight, v_weight, gate_weight, beta_weight, decay_weight, q_conv, k_conv, v_conv, decay_scale, dt_bias, out_gain, out_weight, norm2_gain, ffn_gate, ffn_up, ffn_down, cotangent):
    params = (norm1_gain, q_weight, k_weight, v_weight, gate_weight, beta_weight, decay_weight, q_conv, k_conv, v_conv, decay_scale, dt_bias, out_gain, out_weight, norm2_gain, ffn_gate, ffn_up, ffn_down)
    seq_inputs = block_input.reshape(SEQS, LEN, D)
    seq_cots = cotangent.reshape(SEQS, LEN, D)
    starting = tuple((jnp.zeros(member.shape, jnp.float32) for member in params))

    def per_sequence(totals, pair_in):
        outputs, grad_rows, grads = one_sequence(pair_in[0], pair_in[1], params)
        return (tuple((totals[member] + grads[member] for member in range(18))), (outputs, grad_rows))
    totals, (outputs, grad_rows) = lax.scan(per_sequence, starting, (seq_inputs, seq_cots))
    return (outputs.reshape(TOKENS, D), grad_rows.reshape(TOKENS, D), totals[0], totals[1], totals[2], totals[3], totals[4], totals[5], totals[6], totals[7], totals[8], totals[9], totals[10], totals[11], totals[12], totals[13], totals[14], totals[15], totals[16], totals[17])
```

```python
import functools

import jax
import jax.numpy as jnp
from jax import lax
from jax.experimental import pallas as pl
from jax.experimental.pallas import tpu as pltpu
from jax.sharding import PartitionSpec as P

EPS = 1e-06
BF = jnp.bfloat16
F32 = jnp.float32
KERNELS = True


def dot(left, right, dims=((1,), (0,))):
    return lax.dot_general(left, right, (dims, ((), ())), preferred_element_type=F32)


NN = ((1,), (0,))
NT = ((1,), (1,))
TN = ((0,), (0,))


def mm1(left, right, dims=NN):
    return dot(left.astype(BF), right.astype(BF), dims)


def halves(value):
    high = value.astype(BF)
    return high, (value - high.astype(F32)).astype(BF)


def mm3(left, right, dims=NN):
    lh, ll = left if isinstance(left, tuple) else halves(left)
    rh, rl = right if isinstance(right, tuple) else halves(right)
    return dot(lh, rh, dims) + (dot(lh, rl, dims) + dot(ll, rh, dims))


def sigmoid(value):
    return 1.0 / (1.0 + jnp.exp(-value))


def row_roll(value, by):
    by = by % value.shape[0]
    if by == 0:
        return value
    return pltpu.roll(value, by, 0) if KERNELS else jnp.roll(value, by, 0)


def rows_down(value, by):
    rows = lax.broadcasted_iota(jnp.int32, value.shape, 0)
    return jnp.where(rows >= by, row_roll(value, by), 0.0)


def rows_up(value, by):
    length = value.shape[0]
    rows = lax.broadcasted_iota(jnp.int32, value.shape, 0)
    return jnp.where(rows < length - by, row_roll(value, length - by), 0.0)


def conv(proj, taps):
    count = taps.shape[0]
    total = taps[count - 1 : count] * proj
    for back in range(1, count):
        total = total + taps[count - 1 - back : count - back] * rows_down(proj, back)
    return total


def conv_back(proj, taps, dpre):
    count = taps.shape[0]
    dproj = taps[count - 1 : count] * dpre
    rows = [None] * count
    rows[count - 1] = jnp.sum(dpre * proj, axis=0, keepdims=True)
    for back in range(1, count):
        up = rows_up(dpre, back)
        dproj = dproj + taps[count - 1 - back : count - back] * up
        rows[count - 1 - back] = jnp.sum(up * proj, axis=0, keepdims=True)
    return dproj, rows


def grids(length):
    row = lax.broadcasted_iota(jnp.int32, (length, length), 0)
    col = lax.broadcasted_iota(jnp.int32, (length, length), 1)
    return row, col


def unit_inverse(low, row, col):
    length = low.shape[0]

    def same(bits):
        return jnp.right_shift(row, bits) == jnp.right_shift(col, bits)

    base = jnp.where(same(3), low, 0.0)
    eye = jnp.where(row == col, 1.0, 0.0)
    inv = eye - base
    base_h = halves(base)
    square = mm3(base_h, base_h)
    square_h = halves(square)
    inv = inv + mm3(inv, square_h)
    fourth = mm3(square_h, square_h)
    inv = inv + mm3(inv, fourth)
    bits = 3
    while (1 << bits) < length:
        off = jnp.where(same(bits + 1) & ~same(bits), low, 0.0)
        inv_h = halves(inv)
        inv = inv - mm3(inv_h, mm3(off, inv_h))
        bits += 1
    return inv


def col_of(matrix, at):
    return matrix[:, at : at + 1]


def lanes_of(columns, width):
    length = [c for c in columns if c is not None][0].shape[0]
    lane = lax.broadcasted_iota(jnp.int32, (length, width), 1)
    total = jnp.zeros((length, width), F32)
    for at, column in enumerate(columns):
        if column is not None:
            total = total + jnp.where(lane == at, column, 0.0)
    return total


def decay_terms(ba, pk, n_heads, row, col):
    beta = sigmoid(ba)
    arg = ba + pk[1:2]
    soft = jnp.maximum(arg, 0.0) + jnp.log1p(jnp.exp(-jnp.abs(arg)))
    log_decay = -pk[0:1] * soft
    lower = jnp.where(row >= col, 1.0, 0.0).astype(BF)
    gh = log_decay.astype(BF)
    rest = log_decay - gh.astype(F32)
    gm = rest.astype(BF)
    gl = (rest - gm.astype(F32)).astype(BF)
    cum = dot(lower, gh) + (dot(lower, gm) + dot(lower, gl))
    nt0 = ((0,), (1,))
    cum_rows = dot(gh, lower, nt0) + (dot(gm, lower, nt0) + dot(gl, lower, nt0))
    return beta, soft, arg, cum, cum_rows


def head_matrices(q, k, cum, cum_rows, at, row, col):
    kk = mm1(k, k, NT)
    qk = mm1(q, k, NT)
    within = row >= col
    differ = jnp.where(within, col_of(cum, at) - cum_rows[at : at + 1], 0.0)
    decay = jnp.where(within, jnp.exp(differ), 0.0)
    return kk, qk, decay


def mixer_forward(n_heads, x, gain1, qw, kw, vw, gw, baw, qc, kc, vc, pk, ogain):
    length = x.shape[0]
    key_width = qw.shape[1] // n_heads
    part = vw.shape[0] // n_heads
    xf = x.astype(F32)
    r1 = lax.rsqrt(jnp.mean(xf * xf, axis=1, keepdims=True) + EPS)
    n1 = (xf * r1 * gain1).astype(BF)
    qp = dot(n1, qw)
    kp = dot(n1, kw)
    vp = dot(n1, vw, NT)
    gp = dot(n1, gw, NT)
    ba = dot(n1, baw, NT)
    row, col = grids(length)
    beta, _, _, cum, cum_rows = decay_terms(ba, pk, n_heads, row, col)
    q_pre = conv(qp, qc)
    k_pre = conv(kp, kc)
    v_pre = conv(vp, vc)
    qs = q_pre * sigmoid(q_pre)
    ks = k_pre * sigmoid(k_pre)
    vs = v_pre * sigmoid(v_pre)
    mod = gp * sigmoid(gp) * ogain
    strict = row > col
    outs, news, invs, ys, sums = [], [], [], [], []
    for head in range(n_heads):
        qh = qs[:, head * key_width : (head + 1) * key_width]
        kh = ks[:, head * key_width : (head + 1) * key_width]
        qh = qh * (lax.rsqrt(jnp.sum(qh * qh, axis=1, keepdims=True) + EPS) * key_width**-0.5)
        kh = kh * lax.rsqrt(jnp.sum(kh * kh, axis=1, keepdims=True) + EPS)
        kk, qk, decay = head_matrices(qh, kh, cum, cum_rows, n_heads + head, row, col)
        bh = col_of(beta, head)
        inv = unit_inverse(jnp.where(strict, bh * kk * decay, 0.0), row, col)
        vh = vs[:, head * part : (head + 1) * part]
        new = mm1(inv, bh * vh)
        out = mm1(qk * decay, new)
        outs.append(out)
        news.append(new)
        invs.append(inv)
        ys.append(out * mod[:, head * part : (head + 1) * part])
        sums.append(jnp.sum(out * out, axis=1, keepdims=True))
    tops = [s.astype(BF).astype(F32) for s in sums]
    tail = lanes_of(tops + [s - t for s, t in zip(sums, tops)], 128)
    return qp, kp, vp, gp, ba, outs, news, invs, ys, tail


def forward_kernel(n_heads, x, gain1, qw, kw, vw, gw, baw, qc, kc, vc, pk, ogain,
                   y_out, qp_o, kp_o, vp_o, gp_o, ba_o, o_o, new_o, inv_o):
    part = vw.shape[0] // n_heads
    qp, kp, vp, gp, ba, outs, news, invs, ys, tail = mixer_forward(
        n_heads, x[...], gain1[...], qw[...], kw[...], vw[...], gw[...], baw[...],
        qc[...], kc[...], vc[...], pk[...], ogain[...])
    qp_o[...] = qp
    kp_o[...] = kp
    vp_o[...] = vp
    gp_o[...] = gp
    ba_o[...] = ba
    for head in range(n_heads):
        lanes = slice(head * part, (head + 1) * part)
        y_out[:, lanes] = ys[head].astype(BF)
        o_o[:, lanes] = outs[head]
        new_o[:, lanes] = news[head]
        inv_o[head] = invs[head].astype(BF)
    wide = n_heads * part
    y_out[:, wide : wide + 2 * n_heads] = tail[:, : 2 * n_heads].astype(BF)
    rest = y_out.shape[1] - wide - 2 * n_heads
    y_out[:, wide + 2 * n_heads :] = jnp.zeros((y_out.shape[0], rest), BF)


def call_forward(n_heads, *args):
    x, _, qw, _, vw = args[:5]
    length = x.shape[0]
    keys = qw.shape[1]
    vals = vw.shape[0]
    packed = -(-(vals + 2 * n_heads) // 128) * 128
    shapes = (
        jax.ShapeDtypeStruct((length, packed), BF),
        jax.ShapeDtypeStruct((length, keys), F32),
        jax.ShapeDtypeStruct((length, keys), F32),
        jax.ShapeDtypeStruct((length, vals), F32),
        jax.ShapeDtypeStruct((length, vals), F32),
        jax.ShapeDtypeStruct((length, args[6].shape[0]), F32),
        jax.ShapeDtypeStruct((length, vals), F32),
        jax.ShapeDtypeStruct((length, vals), F32),
        jax.ShapeDtypeStruct((n_heads, length, length), BF),
    )
    return run_kernel(functools.partial(forward_kernel, n_heads), shapes, args, "mixer_forward")


class Slot:
    def __init__(self, shape, dtype):
        self.value = jnp.zeros(shape, dtype)
        self.shape = shape
        self.dtype = dtype

    def __setitem__(self, key, new):
        self.value = self.value.at[key].set(new)


def run_kernel(body, shapes, args, name, flops=1 << 31):
    if not KERNELS:
        slots = [Slot(s.shape, s.dtype) for s in shapes]
        body(*args, *slots)
        return tuple(s.value for s in slots)
    whole = pl.BlockSpec(memory_space=pltpu.VMEM)
    size = sum(a.size * a.dtype.itemsize for a in args)
    size += sum(s.size * s.dtype.itemsize for s in shapes)
    return pl.pallas_call(
        body,
        out_shape=shapes,
        in_specs=[whole] * len(args),
        out_specs=tuple([whole] * len(shapes)),
        name=name,
        compiler_params=pltpu.CompilerParams(vmem_limit_bytes=56 << 20),
        cost_estimate=pl.CostEstimate(flops=flops, bytes_accessed=size, transcendentals=0),
    )(*args)


def head_scales(packed, n_heads, part, groups):
    wide = n_heads * part
    tails = [packed[g][:, wide:].astype(F32) for g in range(groups)]
    total = tails[0]
    for tail in tails[1:]:
        total = total + tail
    scales = []
    for head in range(n_heads):
        square = col_of(total, head) + col_of(total, n_heads + head)
        scales.append(lax.rsqrt(square / (groups * part) + EPS))
    return scales


def mix_kernel(n_heads, y_all, ow, mix_out, z_out):
    groups, wide = ow.shape[0], ow.shape[1]
    part = wide // n_heads
    packed = [y_all[g] for g in range(groups)]
    scales = head_scales(packed, n_heads, part, groups)
    length = packed[0].shape[0]
    lane = lax.broadcasted_iota(jnp.int32, (length, wide), 1)
    scale = jnp.zeros((length, wide), F32)
    for head in range(n_heads):
        inside = (lane >= head * part) & (lane < (head + 1) * part)
        scale = jnp.where(inside, scales[head], scale)
    total = None
    for g in range(groups):
        z = (packed[g][:, :wide].astype(F32) * scale).astype(BF)
        z_out[g] = z
        term = dot(z, ow[g])
        total = term if total is None else total + term
    mix_out[...] = total.astype(BF)


def ffn_kernel(x, mix_a, mix_b, gain2, wg, wu, wd, cot, h_out, n2_out, down_out, dn2_out):
    h = x[...].astype(F32) + (mix_a[...].astype(F32) + mix_b[...].astype(F32))
    r2 = lax.rsqrt(jnp.mean(h * h, axis=1, keepdims=True) + EPS)
    n2 = (h * r2 * gain2[...]).astype(BF)
    h_out[...] = h
    n2_out[...] = n2
    a = dot(n2, wg[...], NT)
    u = dot(n2, wu[...], NT)
    sig = sigmoid(a)
    silu = a * sig
    down_out[...] = dot((silu * u).astype(BF), wd[...]).astype(BF)
    dinner = dot(cot[...], wd[...], NT)
    da = (dinner * u * (sig + silu * (1.0 - sig))).astype(BF)
    du = (dinner * silu).astype(BF)
    dn2_out[...] = (dot(da, wg[...]) + dot(du, wu[...])).astype(BF)


def backward_kernel(n_heads, me, x, gain1, qw, kw, vw, gw, baw, qc, kc, vc, pk, ogain,
                    y_all, ow, dhb, qp_i, kp_i, vp_i, gp_i, ba_i, o_i, new_i, inv_i,
                    m_out, n_out, dn1_out):
    groups, wide = ow.shape[0], ow.shape[1]
    part = wide // n_heads
    length = x.shape[0]
    keys = qw.shape[1]
    key_width = keys // n_heads
    packed = [y_all[g] for g in range(groups)]
    scales = head_scales(packed, n_heads, part, groups)
    dh = dhb[...]
    dz = jnp.zeros((length, wide), F32)
    eo = [jnp.zeros((length, 1), F32) for _ in range(n_heads)]
    mine = me[0, 0] if KERNELS else me[0, 0]
    for g in range(groups):
        dz_g = dot(dh, ow[g], NT)
        dz = dz + jnp.where(mine == g, 1.0, 0.0) * dz_g
        prod = dz_g * packed[g][:, :wide].astype(F32)
        for head in range(n_heads):
            eo[head] = eo[head] + jnp.sum(
                prod[:, head * part : (head + 1) * part], axis=1, keepdims=True)
    row, col = grids(length)
    ba = ba_i[...]
    params = pk[...]
    beta, soft, arg, cum, cum_rows = decay_terms(ba, params, n_heads, row, col)
    qp, kp, vp, gp = qp_i[...], kp_i[...], vp_i[...], gp_i[...]
    q_taps, k_taps, v_taps = qc[...], kc[...], vc[...]
    q_pre = conv(qp, q_taps)
    k_pre = conv(kp, k_taps)
    v_pre = conv(vp, v_taps)
    q_sig, k_sig, v_sig, g_sig = sigmoid(q_pre), sigmoid(k_pre), sigmoid(v_pre), sigmoid(gp)
    qs, ks, vs, gs = q_pre * q_sig, k_pre * k_sig, v_pre * v_sig, gp * g_sig
    out_gain = ogain[...]
    outs = o_i[...]
    news = new_i[...]
    lower = row >= col
    strict = row > col
    ones = jnp.ones((length, 128), BF)
    dqs, dks, dvs, dgs, gain_rows = [], [], [], [], []
    dbetas, dcums = [], []
    for head in range(n_heads):
        lanes = slice(head * part, (head + 1) * part)
        wide_lanes = slice(head * key_width, (head + 1) * key_width)
        o = outs[:, lanes]
        rho = scales[head]
        z_grad = dz[:, lanes]
        gh, gsig, s = gp[:, lanes], g_sig[:, lanes], gs[:, lanes]
        og = out_gain[:, lanes]
        e = z_grad * og * s
        zo = z_grad * o * rho
        gain_rows.append(jnp.sum(zo * s, axis=0, keepdims=True))
        dgs.append(zo * og * (gsig + s * (1.0 - gsig)))
        do = rho * e - o * (rho * rho * rho * eo[head] * (1.0 / (groups * part)))
        qh, kh, vh = qs[:, wide_lanes], ks[:, wide_lanes], vs[:, lanes]
        rq = lax.rsqrt(jnp.sum(qh * qh, axis=1, keepdims=True) + EPS)
        rk = lax.rsqrt(jnp.sum(kh * kh, axis=1, keepdims=True) + EPS)
        qn = qh * (rq * key_width**-0.5)
        kn = kh * rk
        kk, qk, decay = head_matrices(qn, kn, cum, cum_rows, n_heads + head, row, col)
        bh = col_of(beta, head)
        new = news[:, lanes]
        attn = qk * decay
        kd = jnp.where(strict, kk * decay, 0.0)
        dnew = mm1(attn, do, TN)
        dx = mm1(inv_i[head], dnew, TN)
        dattn = jnp.where(lower, mm1(do, new, NT), 0.0)
        dlow = jnp.where(strict, -mm1(dx, new, NT), 0.0)
        dvs.append(bh * dx)
        lowd = dlow * kd
        dbetas.append(jnp.sum(dx * vh, axis=1, keepdims=True)
                      + jnp.sum(lowd, axis=1, keepdims=True))
        pair = dattn * attn + lowd * bh
        ph, pl_ = halves(pair)
        by_col = dot(ph, ones, TN) + dot(pl_, ones, TN)
        dcums.append(jnp.sum(pair, axis=1, keepdims=True) - col_of(by_col, 0))
        dqk = dattn * decay
        dkk = dlow * (bh * decay)
        dq = mm1(dqk, kn)
        dk = mm1(dqk, qn, TN) + mm1(dkk, kn) + mm1(dkk, kn, TN)
        dq = key_width**-0.5 * dq
        dqs.append(rq * dq - qh * (rq * rq * rq * jnp.sum(dq * qh, axis=1, keepdims=True)))
        dks.append(rk * dk - kh * (rk * rk * rk * jnp.sum(dk * kh, axis=1, keepdims=True)))
    width = ba.shape[1]
    dbeta = lanes_of(dbetas, width)
    dcum = lanes_of([None] * n_heads + dcums, width)
    upper = jnp.where(col >= row, 1.0, 0.0).astype(BF)
    ch, cl = halves(dcum)
    dlog = dot(upper, ch) + dot(upper, cl)
    dba = dbeta * beta * (1.0 - beta) - dlog * params[0:1] * sigmoid(arg)
    dscale = -jnp.sum(dlog * soft, axis=0, keepdims=True)
    dbias = -jnp.sum(dlog * params[0:1] * sigmoid(arg), axis=0, keepdims=True)

    def all_back(parts, pre_sig, act, proj, taps):
        dact = jnp.concatenate(parts, axis=1)
        return conv_back(proj, taps, dact * (pre_sig + act * (1.0 - pre_sig)))

    dqp, q_rows = all_back(dqs, q_sig, qs, qp, q_taps)
    dkp, k_rows = all_back(dks, k_sig, ks, kp, k_taps)
    dvp, v_rows = all_back(dvs, v_sig, vs, vp, v_taps)
    dgp = jnp.concatenate(dgs, axis=1)
    dqb, dkb, dvb, dgb, dbb = (t.astype(BF) for t in (dqp, dkp, dvp, dgp, dba))
    dn1 = (dot(dqb, qw[...], NT) + dot(dkb, kw[...], NT) + dot(dvb, vw[...])
           + dot(dgb, gw[...]) + dot(dbb, baw[...]))
    dn1_out[...] = dn1.astype(BF)
    xf = x[...].astype(F32)
    r1 = lax.rsqrt(jnp.mean(xf * xf, axis=1, keepdims=True) + EPS)
    norm_row = jnp.sum(dn1 * (xf * r1), axis=0, keepdims=True)
    m_out[...] = jnp.zeros(m_out.shape, BF)
    m_out[0:length, 0:keys] = dqb
    m_out[0:length, keys : 2 * keys] = dkb
    m_out[0:length, 2 * keys : 2 * keys + width] = dbb
    count = len(q_rows)
    small = jnp.zeros((m_out.shape[0] - length, keys), F32)
    at_row = lax.broadcasted_iota(jnp.int32, small.shape, 0)
    small_q, small_k = small, small
    for tap in range(count):
        small_q = jnp.where(at_row == tap, q_rows[tap], small_q)
        small_k = jnp.where(at_row == tap, k_rows[tap], small_k)
    half = norm_row.shape[1] // 4
    for quarter in range(4):
        piece = norm_row[:, quarter * half : (quarter + 1) * half]
        piece = jnp.concatenate([piece, jnp.zeros((1, keys - half), F32)], axis=1)
        small_q = jnp.where(at_row == 8 + quarter, piece, small_q)
    m_out[length:, 0:keys] = small_q.astype(BF)
    m_out[length:, keys : 2 * keys] = small_k.astype(BF)
    row_w = lax.broadcasted_iota(jnp.int32, (small.shape[0], width), 0)
    sb = jnp.where(row_w == 0, dscale, jnp.where(row_w == 1, dbias, 0.0))
    m_out[length:, 2 * keys : 2 * keys + width] = sb.astype(BF)
    n_out[0:length, :] = jnp.concatenate([dvb, dgb], axis=1)
    gain_row = jnp.concatenate(gain_rows, axis=1)
    small_v = jnp.zeros((n_out.shape[0] - length, wide), F32)
    at_row = lax.broadcasted_iota(jnp.int32, small_v.shape, 0)
    for tap in range(count):
        small_v = jnp.where(at_row == tap, v_rows[tap], small_v)
    small_g = jnp.where(at_row == 0, gain_row, 0.0)
    n_out[length:, :] = jnp.concatenate([small_v, small_g], axis=1).astype(BF)


def call_backward(n_heads, *args):
    x, qw, baw, ow = args[1], args[3], args[7], args[14]
    length, width = x.shape
    keys = qw.shape[1]
    shapes = (
        jax.ShapeDtypeStruct((length + 16, 2 * keys + 128), BF),
        jax.ShapeDtypeStruct((length + 16, 2 * ow.shape[1]), BF),
        jax.ShapeDtypeStruct((length, width), BF),
    )
    body = functools.partial(backward_kernel, n_heads)
    if not KERNELS:
        return run_kernel(body, shapes, args, "mixer_backward")
    whole = pl.BlockSpec(memory_space=pltpu.VMEM)
    return pl.pallas_call(
        body,
        out_shape=shapes,
        in_specs=[pl.BlockSpec(memory_space=pltpu.SMEM)] + [whole] * (len(args) - 1),
        out_specs=tuple([whole] * len(shapes)),
        name="mixer_backward",
        compiler_params=pltpu.CompilerParams(vmem_limit_bytes=56 << 20),
        cost_estimate=pl.CostEstimate(flops=1 << 32, bytes_accessed=1 << 24, transcendentals=0),
    )(*args)


def swap(value, axis, mask):
    count = lax.axis_size(axis)
    return lax.ppermute(value, axis, [(i, i ^ mask) for i in range(count)])


def pair_sum(value, axis):
    count = lax.axis_size(axis)
    if count & (count - 1):
        return lax.psum(value, axis).astype(F32)
    masks = [1 << bit for bit in range(count.bit_length() - 1)]
    half = value.shape[0] // 2
    parts = [value[:half], value[half:]]
    orders = [masks, masks[::-1]]
    total = [p.astype(F32) for p in parts]
    for step in range(len(masks)):
        low = [t.astype(BF) for t in total]
        got = [swap(low[i], axis, orders[i][step]) for i in range(2)]
        total = [low[i].astype(F32) + got[i].astype(F32) for i in range(2)]
    return jnp.concatenate(total, axis=0)


def whole_sequence(rows):
    count = lax.axis_size("seq")
    if count != 2:
        return lax.all_gather(rows, "seq", axis=0, tiled=True)
    other = swap(rows, "seq", 1)
    first = lax.axis_index("seq") == 0
    return jnp.concatenate(
        [jnp.where(first, rows, other), jnp.where(first, other, rows)], axis=0)


def own_rows_sum(partial):
    count = lax.axis_size("seq")
    length = partial.shape[0] // count
    at = lax.axis_index("seq")
    own = lax.dynamic_slice_in_dim(partial, at * length, length, 0)
    if count != 2:
        full = lax.psum_scatter(partial, "seq", scatter_dimension=0, tiled=True)
        return full, jnp.zeros_like(full)
    theirs = lax.dynamic_slice_in_dim(partial, (1 - at) * length, length, 0)
    return own, swap(theirs, "seq", 1)


def on_device(block_input, norm1_gain, q_weight, k_weight, v_weight, gate_weight, beta_weight,
              decay_weight, q_conv, k_conv, v_conv, decay_scale, dt_bias, out_gain, out_weight,
              norm2_gain, ffn_gate, ffn_up, ffn_down, cotangent):
    rows, model = block_input.shape
    all_heads = beta_weight.shape[1]
    seq_size = lax.axis_size("seq")
    n_heads = all_heads // seq_size
    part = v_weight.shape[2]
    keys = q_weight.shape[1] // seq_size
    vals = n_heads * part
    taps = q_conv.shape[0]
    at = lax.axis_index("seq")
    both = ("dp", "seq")

    def gather(value):
        return lax.all_gather(value, both, axis=0)

    vt = jnp.transpose(v_weight, (1, 2, 0)).reshape(all_heads * part, model)
    gt = jnp.transpose(gate_weight, (1, 2, 0)).reshape(all_heads * part, model)
    ot = out_weight.reshape(all_heads * part, model)
    cut = functools.partial(lax.dynamic_slice_in_dim, axis=0)
    ow_own = cut(ot, at * vals, vals)
    ow = lax.all_gather(ow_own, "tensor", axis=0)
    x_all = gather(block_input)
    cot_all = gather(cotangent)
    qw = lax.dynamic_slice_in_dim(q_weight, at * keys, keys, 1)
    kw = lax.dynamic_slice_in_dim(k_weight, at * keys, keys, 1)
    vw = cut(vt, at * vals, vals)
    gw = cut(gt, at * vals, vals)
    bw = cut(beta_weight.T, at * n_heads, n_heads)
    aw = cut(decay_weight.T, at * n_heads, n_heads)
    lanes = 16
    fill = jnp.zeros((lanes - 2 * n_heads, model), BF)
    baw = jnp.concatenate([bw, aw, fill], axis=0)
    qc = lax.dynamic_slice_in_dim(q_conv, at * keys, keys, 1)
    kc = lax.dynamic_slice_in_dim(k_conv, at * keys, keys, 1)
    vc = lax.dynamic_slice_in_dim(v_conv, at * n_heads, n_heads, 1).reshape(taps, vals)
    side = (n_heads, lanes - 2 * n_heads)
    pk = jnp.stack([jnp.pad(cut(decay_scale, at * n_heads, n_heads), side),
                    jnp.pad(cut(dt_bias, at * n_heads, n_heads), side)])
    ogain = jnp.tile(out_gain, n_heads)[None]
    gain1 = norm1_gain[None]
    gain2 = norm2_gain[None]

    x = whole_sequence(block_input)
    params = (x, gain1, qw, kw, vw, gw, baw, qc, kc, vc, pk, ogain)
    y, *saved = call_forward(n_heads, *params)
    y_all = lax.all_gather(y, "tensor", axis=0)
    groups = y_all.shape[0]
    length = x.shape[0]
    mix, z_all = run_kernel(
        functools.partial(mix_kernel, n_heads),
        (jax.ShapeDtypeStruct((length, model), BF),
         jax.ShapeDtypeStruct((groups, length, vals), BF)), (y_all, ow), "mix")
    mix_own, mix_other = own_rows_sum(mix)

    wg, wu = ffn_gate.T, ffn_up.T
    h, n2, down, dn2 = run_kernel(
        ffn_kernel,
        (jax.ShapeDtypeStruct((rows, model), F32), jax.ShapeDtypeStruct((rows, model), BF),
         jax.ShapeDtypeStruct((rows, model), BF), jax.ShapeDtypeStruct((rows, model), BF)),
        (block_input, mix_own, mix_other, gain2, wg, wu, ffn_down, cotangent), "ffn")
    dn2 = pair_sum(dn2, "tensor")
    n2_all = gather(n2)
    r2 = lax.rsqrt(jnp.mean(h * h, axis=1, keepdims=True) + EPS)
    e2 = dn2 * gain2
    norm2_row = jnp.sum(dn2 * h * r2, axis=0)
    dh = cotangent.astype(F32) + r2 * e2 - h * (
        r2 * r2 * r2 * jnp.mean(e2 * h, axis=1, keepdims=True))
    dhb = whole_sequence(dh.astype(BF))
    block_output = (h + pair_sum(down, "tensor")).astype(BF)

    mine = lax.axis_index("tensor").astype(jnp.int32).reshape(1, 1)
    m, n, dn1 = call_backward(n_heads, mine, *params, y_all, ow, dhb, *saved)
    dn1 = pair_sum(sum_pair(own_rows_sum(dn1)), "tensor")
    xf = block_input.astype(F32)
    r1 = lax.rsqrt(jnp.mean(xf * xf, axis=1, keepdims=True) + EPS)
    e1 = dn1 * gain1
    grad_input = dh + (r1 * e1 - xf * (r1 * r1 * r1 * jnp.mean(e1 * xf, axis=1, keepdims=True)))

    n2_rows = n2_all.reshape(-1, model)
    cot_rows = cot_all.reshape(-1, model)
    a = dot(n2_rows, wg, NT)
    u = dot(n2_rows, wu, NT)
    sig = sigmoid(a)
    silu = a * sig
    dinner = dot(cot_rows, ffn_down, NT)
    inner = (silu * u).astype(BF)
    da = (dinner * u * (sig + silu * (1.0 - sig))).astype(BF)
    du = (dinner * silu).astype(BF)
    grad_gate = dot(da, n2_rows, TN).T
    grad_up = dot(du, n2_rows, TN).T
    grad_down = dot(inner, cot_rows, TN)

    xa = x_all.reshape(-1, model).astype(F32)
    n1_rows = (xa * lax.rsqrt(jnp.mean(xa * xa, axis=1, keepdims=True) + EPS) * gain1).astype(BF)
    n1_rows = n1_rows.reshape(-1, length, model)

    me_t = lax.axis_index("tensor")
    z_own = lax.dynamic_index_in_dim(z_all, me_t, 0, keepdims=False)
    out_part = dot(z_own, dhb, TN).astype(BF)
    out_sum = lax.psum(out_part, "dp")
    grad_out = whole_sequence(out_sum).astype(F32).reshape(out_weight.shape)

    n_full = gather(jnp.concatenate(
        [n, jnp.pad(norm2_row.reshape(-1, 256), ((0, 12), (0, n.shape[1] - 256))).astype(BF)],
        axis=0))
    n_full = n_full.reshape((-1, seq_size) + n_full.shape[1:])
    dvg = n_full[:, :, :length]
    n_small = jnp.sum(n_full[:, :, length:].astype(F32), axis=0)
    grad_v, grad_g = [], []
    for s in range(seq_size):
        d = lax.dot_general(dvg[:, s], n1_rows, (((0, 1), (0, 1)), ((), ())),
                            preferred_element_type=F32)
        grad_v.append(d[:vals])
        grad_g.append(d[vals:])
    shape3 = (all_heads, part, model)
    grad_v = jnp.transpose(jnp.concatenate(grad_v, axis=0).reshape(shape3), (2, 0, 1))
    grad_g = jnp.transpose(jnp.concatenate(grad_g, axis=0).reshape(shape3), (2, 0, 1))
    grad_vc = jnp.transpose(n_small[:, :taps, :vals].reshape(seq_size, taps, n_heads, part),
                            (1, 0, 2, 3)).reshape(v_conv.shape)
    grad_gain = jnp.sum(n_small[:, 0, vals:].reshape(-1, part), axis=0)
    grad_norm2 = jnp.sum(n_small[:, 16:20, :256], axis=0).reshape(-1)

    m_full = gather(pair_sum(m, "tensor").astype(BF))
    m_full = m_full.reshape((-1, seq_size) + m_full.shape[1:])
    m_small = jnp.sum(m_full[:, :, length:].astype(F32), axis=0)
    grad_q, grad_k, grad_b, grad_a = [], [], [], []
    for s in range(seq_size):
        for lo, out in ((0, grad_q), (keys, grad_k)):
            out.append(lax.dot_general(n1_rows, m_full[:, s, :length, lo : lo + keys],
                                       (((0, 1), (0, 1)), ((), ())), preferred_element_type=F32))
        d = lax.dot_general(m_full[:, s, :length, 2 * keys : 2 * keys + lanes], n1_rows,
                            (((0, 1), (0, 1)), ((), ())), preferred_element_type=F32)
        grad_b.append(d[:n_heads])
        grad_a.append(d[n_heads : 2 * n_heads])
    grad_q = jnp.concatenate(grad_q, axis=1)
    grad_k = jnp.concatenate(grad_k, axis=1)
    grad_b = jnp.concatenate(grad_b, axis=0).T
    grad_a = jnp.concatenate(grad_a, axis=0).T
    grad_qc = jnp.transpose(m_small[:, :taps, :keys], (1, 0, 2)).reshape(q_conv.shape)
    grad_kc = jnp.transpose(m_small[:, :taps, keys : 2 * keys], (1, 0, 2)).reshape(k_conv.shape)
    first = 2 * keys + n_heads
    grad_scale = m_small[:, 0, first : first + n_heads].reshape(-1)
    grad_bias = m_small[:, 1, first : first + n_heads].reshape(-1)
    grad_norm1 = jnp.sum(m_small[:, 8:12, : model // 4], axis=0).reshape(-1)
    return (block_output, grad_input, grad_norm1, grad_q, grad_k, grad_v, grad_g, grad_b, grad_a,
            grad_qc, grad_kc, grad_vc, grad_scale, grad_bias, grad_gain, grad_out, grad_norm2,
            grad_gate, grad_up, grad_down)


def sum_pair(pair):
    return (pair[0].astype(F32) + pair[1].astype(F32)).astype(BF)


def solution(mesh):
    rows = P(("dp", "seq"), None)
    third = P(None, None, "tensor")
    second = P(None, "tensor")
    first = P("tensor", None)
    middle = P(None, "tensor", None)
    placed = (rows, P(), P(), P(), third, third, P(), P(), P(), P(), third, P(), P(),
              P("tensor"), middle, P(), second, second, first, rows)
    outs = (rows, rows, P(), P(), P(), third, third, P(), P(), P(), P(), third, P(), P(),
            P("tensor"), middle, P(), second, second, first)
    return jax.shard_map(on_device, mesh=mesh, in_specs=placed, out_specs=outs, check_vma=False)
```
